32 devices in a mesh: inst: 2 (over core), pipe: 4 (over z), tensor: 4 (over y, x).
Axes of the slice: x: 2, y: 2, z: 4, core: 2. Of those that a mesh axis runs over, the one named last changes fastest.
Arguments:
- lengths: int32 [2, 64], replicated, may hold values from 2 to 384, as said below
- page_table: int32 [2, 64, 3], P('inst'), may hold values from 0 to 191, as said below
- migration: int32 [16, 3], replicated, may hold values from 0 to 63, as said below
- dest_slots: int32 [16, 3], replicated, may hold values from 0 to 47, as said below
- queries: bfloat16 [2, 4, 64, 8192], P('inst', 'pipe', None, 'tensor'), may hold values from -64 to 64
- key_cache: bfloat16 [2, 4, 8, 24576, 128], P('inst', 'pipe', 'tensor'), may hold values from -64 to 64
- value_cache: bfloat16 [2, 4, 8, 24576, 128], P('inst', 'pipe', 'tensor'), may hold values from -5 to 5
- out_weight: bfloat16 [4, 8192, 8192], P('pipe', 'tensor'), may hold values from -0.09375 to 0.09375
Outputs:
- update: bfloat16 [2, 64, 8192], P('inst', None, ('pipe', 'tensor'))
- received_keys: bfloat16 [2, 4, 8, 6144, 128], P('inst', 'pipe', 'tensor')
- received_values: bfloat16 [2, 4, 8, 6144, 128], P('inst', 'pipe', 'tensor')
The draws below stay inside these ranges and needn't reach their ends.
Inputs may be any that keep to these rules, and one draw needn't show every extreme that they name: `lengths`: in instance 1 every request holds more than 192 tokens and one holds exactly 384; in instance 0 every request holds at most 192. `page_table`: for each instance a permutation of its 192 pool pages, 3 for each request. `migration`: rows 0 to 7 name source instance 1 and destination instance 0, the other rows source 0 and destination 1; the requests of all rows are distinct numbers, and the one in row 0 holds at most (2) * 128 tokens. `dest_slots`: A permutation of the 48 receive slots.
All inputs are finite; a program needn't handle non-finite values.
Results may differ from the reference program's by a relative error of at most 0.018.
Values may be sent and summed in bfloat16 or wider, within the bound.
A program may use at most 128 MiB of HBM per device.

```python
import math
import jax
import jax.numpy as jnp
from jax import lax

D = 8192
HEADS = 64
KVH = 8
HD = 128
PAGE = 128
MAXP = 3
ROWS = 64
LAYERS = 4
MOVE = 16
POOL = 192
RECV = 48
N_INST = 2


def layout(key):
    base_key = jax.random.fold_in(key, 11)
    subkeys = jax.random.split(base_key, 7)
    full_length = MAXP * PAGE
    half_length = full_length // 2
    heavy_side = 1
    half_move = MOVE // 2
    order = jax.random.permutation(subkeys[4], ROWS)
    chosen = order[:MOVE]
    longest_row = order[ROWS - 1]
    long_lengths = jax.random.randint(subkeys[1], (ROWS,), half_length + 1, full_length + 1)
    first_length = jax.random.randint(subkeys[2], (), half_length + 1, (MAXP - 1) * PAGE + 1)
    long_lengths = jnp.where(jnp.arange(ROWS) == chosen[0], first_length, long_lengths)
    long_lengths = jnp.where(jnp.arange(ROWS) == longest_row, full_length, long_lengths)
    short_lengths = jax.random.randint(subkeys[3], (ROWS,), 2, half_length + 1)
    is_heavy = (jnp.arange(N_INST) == heavy_side)[:, None]
    lengths = jnp.where(is_heavy, long_lengths[None, :], short_lengths[None, :]).astype(jnp.int32)
    from_heavy = jnp.arange(MOVE) < half_move
    source_col = jnp.where(from_heavy, heavy_side, 1 - heavy_side)
    target_col = 1 - source_col
    migration = jnp.stack([chosen, source_col, target_col], axis=1).astype(jnp.int32)
    table_keys = jax.random.split(subkeys[5], N_INST)
    page_table = jnp.stack([jax.random.permutation(table_keys[index], POOL) for index in range(N_INST)]).reshape(N_INST, ROWS, MAXP).astype(jnp.int32)
    dest_slots = jax.random.permutation(subkeys[6], RECV).reshape(MOVE, MAXP).astype(jnp.int32)
    return (lengths, page_table, migration, dest_slots)


def draw_lengths(key, part):
    return layout(key)[0]


def draw_page_table(key, part):
    return layout(key)[1]


def draw_migration(key, part):
    return layout(key)[2]


def draw_dest_slots(key, part):
    return layout(key)[3]


def draw_queries(key, part):
    drawn = jnp.clip(jax.random.normal(jax.random.fold_in(key, 41), (N_INST, LAYERS, ROWS, HEADS * HD), jnp.float32), -4.0, 4.0)
    return drawn.astype(jnp.bfloat16)


def draw_key_cache(key, part):
    drawn = jnp.clip(jax.random.normal(jax.random.fold_in(key, 21), (N_INST, LAYERS, KVH, POOL * PAGE, HD), jnp.float32), -4.0, 4.0)
    return drawn.astype(jnp.bfloat16)


def raised(entries, key, source, target, blocks, factor):
    owner, partner = [(jnp.arange(entries.shape[axis_at]) // (entries.shape[axis_at] // blocks)).reshape([-1 if axis == axis_at else 1 for axis in range(entries.ndim)]) for axis_at in (source, target)]
    chosen = jax.random.permutation(key, blocks)[partner]
    strong = (owner == chosen) | (owner == (partner + blocks // 2) % blocks)
    return jnp.where(strong, factor * entries, entries)


def block_scale(stream_key, dims, cuts, low, high):
    def one(dim, shards_of):
        steps = jax.random.uniform(jax.random.fold_in(jax.random.fold_in(stream_key, 6), dim), (shards_of,), jnp.float32, low / len(cuts), high / len(cuts))
        return jnp.repeat(jnp.exp(steps), dims[dim] // shards_of).reshape((-1,) + (1,) * (len(dims) - dim - 1))

    gain = one(*cuts[0])
    for cut in cuts[1:]:
        gain = gain * one(*cut)
    return gain


def gaussian(stream_key, shape, spread, most, shards=(), kind=jnp.bfloat16):
    drawn = spread * jax.random.normal(stream_key, shape, jnp.float32)
    if shards:
        drawn = drawn * block_scale(stream_key, shape, shards, -0.22, 0.18)
    return jnp.clip(drawn, -most, most).astype(kind)


def heavy_noise(key, dims, deviation, bound, shards, heavy, kind=jnp.bfloat16):
    values = deviation * jax.random.normal(key, dims, jnp.float32)
    if shards:
        values = values * block_scale(key, dims, shards, -0.22, 0.18)
    return jnp.clip(raised(values, jax.random.fold_in(key, 3), *heavy), -bound, bound).astype(kind)


def setup_inputs(seed: int = 0) -> dict:
    keys = jax.random.split(jax.random.key(seed), 9)
    lengths = draw_lengths(jax.random.fold_in(keys[8], 71), 0)
    page_table = draw_page_table(jax.random.fold_in(keys[8], 71), 0)
    migration = draw_migration(jax.random.fold_in(keys[8], 71), 0)
    dest_slots = draw_dest_slots(jax.random.fold_in(keys[8], 71), 0)
    queries = draw_queries(jax.random.fold_in(keys[8], 71), 0)
    key_cache = draw_key_cache(jax.random.fold_in(keys[8], 71), 0)
    value_cache = gaussian(keys[6], (N_INST, LAYERS, KVH, POOL * PAGE, HD), 1.0, 5.0, ((0, 2), (1, 4), (2, 4)))
    out_weight = heavy_noise(keys[7], (LAYERS, HEADS * HD, D), (HEADS * HD) ** -0.5, 0.09375, ((0, 4), (1, 4)), (1, 2, 4, 2.0))
    return dict(lengths=lengths, page_table=page_table, migration=migration, dest_slots=dest_slots, queries=queries, key_cache=key_cache, value_cache=value_cache, out_weight=out_weight)


def attend_all(query_rows, key_rows, value_rows, page_map, length_list):
    group_size = HEADS // KVH
    scale_factor = 1.0 / math.sqrt(HD)
    key_pages = key_rows.reshape(KVH, POOL, PAGE, HD)
    value_pages = value_rows.reshape(KVH, POOL, PAGE, HD)
    gathered_keys = key_pages[:, page_map].reshape(KVH, ROWS, MAXP * PAGE, HD).astype(jnp.float32)
    gathered_values = value_pages[:, page_map].reshape(KVH, ROWS, MAXP * PAGE, HD).astype(jnp.float32)
    query_split = query_rows.reshape(ROWS, KVH, group_size, HD).astype(jnp.float32)
    scores = jnp.einsum('rkgd,krtd->rkgt', query_split, gathered_keys, precision=lax.Precision.HIGHEST) * scale_factor
    position = jnp.arange(MAXP * PAGE, dtype=jnp.int32)
    visible = position[None, :] < length_list[:, None]
    scores = jnp.where(visible[:, None, None, :], scores, -jnp.inf)
    weights = jax.nn.softmax(scores, axis=-1)
    attended = jnp.einsum('rkgt,krtd->rkgd', weights, gathered_values, precision=lax.Precision.HIGHEST)
    return attended.reshape(ROWS, HEADS * HD).astype(jnp.bfloat16)

def reference(lengths, page_table, migration, dest_slots, queries, key_cache, value_cache, out_weight):

    def one_layer(flat_index):
        instance = flat_index // LAYERS
        layer_index = flat_index % LAYERS
        attended = attend_all(queries[instance, layer_index], key_cache[instance, layer_index], value_cache[instance, layer_index], page_table[instance], lengths[instance])
        return jnp.dot(attended, out_weight[layer_index], preferred_element_type=jnp.float32)
    layer_terms = lax.map(one_layer, jnp.arange(N_INST * LAYERS, dtype=jnp.int32))
    update = lax.optimization_barrier(jnp.sum(layer_terms.reshape(N_INST, LAYERS, ROWS, D), axis=1)).astype(jnp.bfloat16)
    movers = migration[:, 0]
    sources = migration[:, 1]
    targets = migration[:, 2]
    moved_lengths = lengths[sources, movers]
    live_pages = (jnp.arange(MAXP, dtype=jnp.int32)[None, :] * PAGE < moved_lengths[:, None]).reshape(-1)
    slot_ids = page_table[sources, movers].reshape(-1)
    source_rep = jnp.repeat(sources, MAXP)
    target_rep = jnp.repeat(targets, MAXP)
    recv_ids = dest_slots.reshape(-1)

    def place(cache_array):
        pages_all = cache_array.reshape(N_INST, LAYERS, KVH, POOL, PAGE, HD)
        moved_pages = pages_all[source_rep, :, :, slot_ids]
        areas = []
        for target in range(N_INST):
            keep = live_pages & (target_rep == target)
            kept = jnp.where(keep[:, None, None, None, None], moved_pages, jnp.zeros_like(moved_pages))
            areas.append(jnp.zeros((RECV, LAYERS, KVH, PAGE, HD), cache_array.dtype).at[recv_ids].set(kept))
        everything = jnp.stack(areas).transpose(0, 2, 3, 1, 4, 5)
        return everything.reshape(N_INST, LAYERS, KVH, RECV * PAGE, HD)
    return (update, place(key_cache), place(value_cache))
```

```python
import functools
import math

import jax
import jax.numpy as jnp
from jax import lax
from jax.experimental import pallas as pl
from jax.experimental.pallas import tpu as pltpu
from jax.sharding import PartitionSpec as P

PAGE = 128
SLOTS = 16
UNROLL = 2
MESH = pl.DeviceIdType.MESH


def from_partner(array, axis, stride):
    return lax.ppermute(array, axis, [(i, i ^ 1 << stride) for i in range(lax.axis_size(axis))])


def attend_kernel(
    length_ref, table_ref, migration_ref, dest_ref, query_ref, key_ref, value_ref,
    out_ref, key_area, value_area,
    key_buf, value_buf, move_buf, zero_buf, page_sem, move_sem,
):
    rows, max_pages = table_ref.shape
    moves = migration_ref.shape[0]
    kv_heads, _, page, head_dim = key_ref.shape
    heads = query_ref.shape[1]
    group = heads // kv_heads
    tokens = max_pages * page
    scale = 1.0 / math.sqrt(head_dim)
    me = lax.axis_index("inst")

    def page_copies(row, index):
        slot = lax.rem(row, SLOTS)
        source = table_ref[row, index]
        place = pl.ds(index * page, page)
        return (
            pltpu.make_async_copy(
                key_ref.at[:, source], key_buf.at[slot, :, place], page_sem.at[slot, index, 0]
            ),
            pltpu.make_async_copy(
                value_ref.at[:, source], value_buf.at[slot, :, place], page_sem.at[slot, index, 1]
            ),
        )

    def each_page(row, act):
        for index in range(max_pages):
            @pl.when(index * page < length_ref[me, row])
            def _():
                for copy in page_copies(row, index):
                    act(copy)

    def each_move(act):
        @pl.loop(0, moves)
        def _(move):
            row, source = migration_ref[move, 0], migration_ref[move, 1]
            for index in range(max_pages):
                live = (source == me) & (index * page < length_ref[source, row])
                slot = dest_ref[move, index]
                act(move, index, live, table_ref[row, index], slot)

    def load_move(move, index, pool_page):
        return [
            pltpu.make_async_copy(
                ref.at[:, pool_page], move_buf.at[move, index, which], move_sem.at[move, index, which]
            )
            for which, ref in enumerate((key_ref, value_ref))
        ]

    def store_move(move, index, slot):
        return [
            pltpu.make_async_copy(
                move_buf.at[move, index, which], area.at[:, slot], move_sem.at[move, index, which]
            )
            for which, area in enumerate((key_area, value_area))
        ]

    def clear_move(move, index, slot):
        return [
            pltpu.make_async_copy(zero_buf, area.at[:, slot], move_sem.at[move, index, which])
            for which, area in enumerate((key_area, value_area))
        ]

    zero_buf[...] = jnp.zeros_like(zero_buf)

    @pl.loop(0, SLOTS)
    def _(slot):
        value_buf[slot] = jnp.zeros(value_buf.shape[1:], value_buf.dtype)

    @pl.loop(0, SLOTS)
    def _(row):
        each_page(row, lambda copy: copy.start())

    def begin_move(move, index, live, pool_page, slot):
        @pl.when(live)
        def _():
            for copy in load_move(move, index, pool_page):
                copy.start()

        @pl.when(jnp.logical_not(live))
        def _():
            for copy in clear_move(move, index, slot):
                copy.start()

    each_move(begin_move)

    position = lax.broadcasted_iota(jnp.int32, (heads, tokens), 1)

    def attend_row(row):
        slot = lax.rem(row, SLOTS)
        keys = key_buf[slot].reshape(kv_heads * tokens, head_dim)
        values = value_buf[slot].reshape(kv_heads * tokens, head_dim)
        full = lax.dot_general(
            query_ref[row], keys, (((1,), (1,)), ((), ())), preferred_element_type=jnp.float32
        )
        scores = jnp.concatenate(
            [
                full[k * group : (k + 1) * group, k * tokens : (k + 1) * tokens]
                for k in range(kv_heads)
            ],
            axis=0,
        )
        scores = jnp.where(position < length_ref[me, row], scores * scale, -1e30)
        weights = jnp.exp(scores - jnp.max(scores, axis=-1, keepdims=True))
        total = jnp.sum(weights, axis=-1, keepdims=True)
        nothing = jnp.zeros((group, tokens), jnp.float32)
        spread = jnp.concatenate(
            [
                jnp.concatenate(
                    [
                        weights[k * group : (k + 1) * group] if at == k else nothing
                        for at in range(kv_heads)
                    ],
                    axis=1,
                )
                for k in range(kv_heads)
            ],
            axis=0,
        )
        mixed = jnp.dot(
            spread.astype(jnp.bfloat16), values, preferred_element_type=jnp.float32
        )
        return (mixed / total).astype(out_ref.dtype)

    steps = rows // UNROLL

    @pl.loop(0, steps)
    def _(step):
        for u in range(UNROLL):
            each_page(step * UNROLL + u, lambda copy: copy.wait())
        results = [attend_row(step * UNROLL + u) for u in range(UNROLL)]
        for u in range(UNROLL):
            out_ref[step * UNROLL + u] = results[u]
        for u in range(UNROLL):
            @pl.when(step * UNROLL + u + SLOTS < rows)
            def _():
                each_page(step * UNROLL + u + SLOTS, lambda copy: copy.start())

        @pl.when(step == steps // 2)
        def _():
            def turn_move(move, index, live, pool_page, slot):
                @pl.when(live)
                def _():
                    for copy in load_move(move, index, pool_page):
                        copy.wait()
                    for copy in store_move(move, index, slot):
                        copy.start()

            each_move(turn_move)

    def end_move(move, index, live, pool_page, slot):
        for copy in clear_move(move, index, slot):
            copy.wait()

    each_move(end_move)


def attend(lengths, page_table, migration, dest_slots, queries, key_pages, value_pages):
    rows, max_pages = page_table.shape
    moves = migration.shape[0]
    kv_heads, _, page, head_dim = key_pages.shape
    heads = queries.shape[1]
    area = jax.ShapeDtypeStruct((kv_heads, moves * max_pages, page, head_dim), key_pages.dtype)
    smem = pl.BlockSpec(memory_space=pltpu.SMEM)
    vmem = pl.BlockSpec(memory_space=pltpu.VMEM)
    hbm = pl.BlockSpec(memory_space=pl.ANY)
    return pl.pallas_call(
        attend_kernel,
        out_shape=(jax.ShapeDtypeStruct(queries.shape, queries.dtype), area, area),
        in_specs=[smem] * 4 + [vmem, hbm, hbm],
        out_specs=(vmem, hbm, hbm),
        scratch_shapes=[
            pltpu.VMEM((SLOTS, kv_heads, max_pages * page, head_dim), key_pages.dtype),
            pltpu.VMEM((SLOTS, kv_heads, max_pages * page, head_dim), key_pages.dtype),
            pltpu.VMEM((moves, max_pages, 2, kv_heads, page, head_dim), key_pages.dtype),
            pltpu.VMEM((kv_heads, page, head_dim), key_pages.dtype),
            pltpu.SemaphoreType.DMA((SLOTS, max_pages, 2)),
            pltpu.SemaphoreType.DMA((moves, max_pages, 2)),
        ],
        name="attend",
    )(lengths, page_table, migration, dest_slots, queries, key_pages, value_pages)


def project_kernel(
    pipes, tensors, attended_ref, weight_ref, out_ref,
    weight_buf, send_one, recv_one, own, send_two, recv_two,
    weight_sem, send_one_sem, recv_one_sem, send_two_sem, recv_two_sem,
):
    my_pipe = lax.axis_index("pipe")
    my_tensor = lax.axis_index("tensor")
    blocks = pipes * tensors
    width = out_ref.shape[1]

    def target(block):
        chunk, turn = block // tensors, lax.rem(block, tensors)
        to_pipe = lax.rem(my_pipe + pipes - 1 - chunk, pipes)
        to_tensor = lax.rem(my_tensor + 1 + turn, tensors)
        return chunk, turn, to_pipe, to_tensor

    def weight_copy(block):
        _, _, to_pipe, to_tensor = target(block)
        start = pl.multiple_of((to_pipe * tensors + to_tensor) * width, width)
        return pltpu.make_async_copy(
            weight_ref.at[:, pl.ds(start, width)], weight_buf.at[block], weight_sem.at[block]
        )

    def first_copy(chunk, turn, to_tensor):
        return pltpu.make_async_remote_copy(
            src_ref=send_one.at[chunk, turn],
            dst_ref=recv_one.at[chunk, turn],
            send_sem=send_one_sem.at[chunk, turn],
            recv_sem=recv_one_sem.at[chunk, turn],
            device_id={"tensor": to_tensor},
            device_id_type=MESH,
        )

    def second_copy(chunk, to_pipe):
        return pltpu.make_async_remote_copy(
            src_ref=send_two.at[chunk],
            dst_ref=recv_two.at[chunk],
            send_sem=send_two_sem.at[chunk],
            recv_sem=recv_two_sem.at[chunk],
            device_id={"pipe": to_pipe},
            device_id_type=MESH,
        )

    @pl.loop(0, blocks)
    def _(block):
        weight_copy(block).start()

    barrier = pltpu.get_barrier_semaphore()
    for step in range(1, tensors):
        pl.semaphore_signal(
            barrier, inc=1, device_id={"tensor": lax.rem(my_tensor + step, tensors)},
            device_id_type=MESH,
        )
    for step in range(1, pipes):
        pl.semaphore_signal(
            barrier, inc=1, device_id={"pipe": lax.rem(my_pipe + step, pipes)},
            device_id_type=MESH,
        )
    pl.semaphore_wait(barrier, tensors + pipes - 2)

    def gathered(chunk):
        total = own[chunk]
        for turn in range(tensors - 1):
            first_copy(chunk, turn, my_tensor).wait_recv()
            total = total + recv_one[chunk, turn].astype(jnp.float32)
        return total

    @pl.loop(0, blocks)
    def _(block):
        chunk, turn, _, to_tensor = target(block)
        weight_copy(block).wait()
        term = jnp.dot(
            attended_ref[...], weight_buf[block], preferred_element_type=jnp.float32
        )

        @pl.when(turn < tensors - 1)
        def _():
            send_one[chunk, turn] = term.astype(send_one.dtype)
            first_copy(chunk, turn, to_tensor).start()

        @pl.when(turn == tensors - 1)
        def _():
            own[chunk] = term

        @pl.when((turn == tensors - 1) & (chunk > 0))
        def _():
            before = chunk - 1
            send_two[before] = gathered(before).astype(send_two.dtype)
            second_copy(before, lax.rem(my_pipe + pipes - 1 - before, pipes)).start()

    total = gathered(pipes - 1)
    for chunk in range(pipes - 1):
        second_copy(chunk, my_pipe).wait_recv()
        total = total + recv_two[chunk].astype(jnp.float32)
    out_ref[...] = total.astype(out_ref.dtype)

    for chunk in range(pipes):
        for turn in range(tensors - 1):
            first_copy(chunk, turn, my_tensor).wait_send()
    for chunk in range(pipes - 1):
        second_copy(chunk, my_pipe).wait_send()


def project(attended, weight):
    pipes, tensors = lax.axis_size("pipe"), lax.axis_size("tensor")
    rows, depth = attended.shape
    columns = weight.shape[1]
    width = columns // (pipes * tensors)
    return pl.pallas_call(
        functools.partial(project_kernel, pipes, tensors),
        out_shape=jax.ShapeDtypeStruct((rows, width), jnp.bfloat16),
        in_specs=[pl.BlockSpec(memory_space=pltpu.VMEM), pl.BlockSpec(memory_space=pl.ANY)],
        out_specs=pl.BlockSpec(memory_space=pltpu.VMEM),
        scratch_shapes=[
            pltpu.VMEM((pipes * tensors, depth, width), weight.dtype),
            pltpu.VMEM((pipes, tensors - 1, rows, width), jnp.bfloat16),
            pltpu.VMEM((pipes, tensors - 1, rows, width), jnp.bfloat16),
            pltpu.VMEM((pipes, rows, width), jnp.float32),
            pltpu.VMEM((pipes - 1, rows, width), jnp.bfloat16),
            pltpu.VMEM((pipes - 1, rows, width), jnp.bfloat16),
            pltpu.SemaphoreType.DMA((pipes * tensors,)),
            pltpu.SemaphoreType.DMA((pipes, tensors - 1)),
            pltpu.SemaphoreType.DMA((pipes, tensors - 1)),
            pltpu.SemaphoreType.DMA((pipes - 1,)),
            pltpu.SemaphoreType.DMA((pipes - 1,)),
        ],
        cost_estimate=pl.CostEstimate(
            flops=2 * rows * depth * columns,
            bytes_accessed=2 * depth * columns,
            transcendentals=0,
        ),
        compiler_params=pltpu.CompilerParams(
            collective_id=0, has_side_effects=True, vmem_limit_bytes=48 * 1024 * 1024
        ),
        name="project",
    )(attended, weight)


def body(lengths, page_table, migration, dest_slots, queries, key_cache, value_cache, out_weight):
    kv_heads = key_cache.shape[2]
    head_dim = key_cache.shape[4]
    row_count = page_table.shape[1]
    pool_pages = key_cache.shape[3] // PAGE
    heads = queries.shape[3] // head_dim
    key_pages = key_cache[0, 0].reshape(kv_heads, pool_pages, PAGE, head_dim)
    value_pages = value_cache[0, 0].reshape(kv_heads, pool_pages, PAGE, head_dim)
    query_block = queries[0, 0].reshape(row_count, heads, head_dim)
    attended, key_area, value_area = attend(
        lengths, page_table[0], migration, dest_slots, query_block, key_pages, value_pages
    )
    got_keys, got_values = from_partner((key_area, value_area), "inst", 0)
    update = project(attended.reshape(row_count, heads * head_dim), out_weight[0])
    shape = (1, 1, kv_heads, got_keys.shape[1] * PAGE, head_dim)
    return (update[None], got_keys.reshape(shape), got_values.reshape(shape))


def solution(mesh):
    placed = (
        P(),
        P("inst", None, None),
        P(),
        P(),
        P("inst", "pipe", None, "tensor"),
        P("inst", "pipe", "tensor", None, None),
        P("inst", "pipe", "tensor", None, None),
        P("pipe", "tensor", None),
    )
    return jax.shard_map(
        body,
        mesh=mesh,
        in_specs=placed,
        out_specs=(
            P("inst", None, ("pipe", "tensor")),
            P("inst", "pipe", "tensor", None, None),
            P("inst", "pipe", "tensor", None, None),
        ),
        check_vma=False,
    )
```

```python
import functools
import math

import jax
import jax.numpy as jnp
from jax import lax
from jax.experimental import pallas as pl
from jax.experimental.pallas import tpu as pltpu
from jax.sharding import PartitionSpec as P

PAGE = 128
SLOTS = 16
UNROLL = 4
MESH = pl.DeviceIdType.MESH


def from_partner(array, axis, stride):
    return lax.ppermute(array, axis, [(i, i ^ 1 << stride) for i in range(lax.axis_size(axis))])


def attend_kernel(
    length_ref, table_ref, migration_ref, dest_ref, query_ref, key_ref, value_ref,
    out_ref, key_area, value_area,
    key_buf, value_buf, move_buf, zero_buf, query_buf, out_buf, page_sem, move_sem,
):
    max_pages, _, rows = table_ref.shape
    moves = migration_ref.shape[1]
    kv_heads, _, page, head_dim = key_ref.shape
    heads = query_ref.shape[1] // head_dim
    group = heads // kv_heads
    tokens = max_pages * page
    scale = 1.0 / math.sqrt(head_dim)
    me = lax.axis_index("inst")

    def page_copies(row, index):
        slot = lax.rem(row, SLOTS)
        source = table_ref[index, 0, row]
        place = pl.ds(index * page, page)
        return (
            pltpu.make_async_copy(
                key_ref.at[:, source], key_buf.at[slot, :, place], page_sem.at[slot, index, 0]
            ),
            pltpu.make_async_copy(
                value_ref.at[:, source], value_buf.at[slot, :, place], page_sem.at[slot, index, 1]
            ),
        )

    def each_page(row, act):
        for index in range(max_pages):
            @pl.when(index * page < length_ref[me, row])
            def _():
                for copy in page_copies(row, index):
                    act(copy)

    def each_move(act):
        @pl.loop(0, moves)
        def _(move):
            row, source = migration_ref[0, move], migration_ref[1, move]
            for index in range(max_pages):
                live = (source == me) & (index * page < length_ref[source, row])
                slot = dest_ref[index, move]
                act(move, index, live, table_ref[index, 0, row], slot)

    def load_move(move, index, pool_page):
        return [
            pltpu.make_async_copy(
                ref.at[:, pool_page], move_buf.at[move, index, which], move_sem.at[move, index, which]
            )
            for which, ref in enumerate((key_ref, value_ref))
        ]

    def store_move(move, index, slot):
        return [
            pltpu.make_async_copy(
                move_buf.at[move, index, which], area.at[:, slot], move_sem.at[move, index, which]
            )
            for which, area in enumerate((key_area, value_area))
        ]

    def clear_move(move, index, slot):
        return [
            pltpu.make_async_copy(zero_buf, area.at[:, slot], move_sem.at[move, index, which])
            for which, area in enumerate((key_area, value_area))
        ]

    zero_buf[...] = jnp.zeros_like(zero_buf)

    @pl.loop(0, SLOTS)
    def _(slot):
        value_buf[slot] = jnp.zeros(value_buf.shape[1:], value_buf.dtype)

    @pl.loop(0, SLOTS)
    def _(row):
        each_page(row, lambda copy: copy.start())

    def begin_move(move, index, live, pool_page, slot):
        @pl.when(live)
        def _():
            for copy in load_move(move, index, pool_page):
                copy.start()

        @pl.when(jnp.logical_not(live))
        def _():
            for copy in clear_move(move, index, slot):
                copy.start()

    each_move(begin_move)

    query_buf[...] = jnp.zeros_like(query_buf)
    for head in range(heads):
        own = head // group * head_dim
        query_buf[:, head, own : own + head_dim] = query_ref[
            :, head * head_dim : (head + 1) * head_dim
        ].astype(jnp.float32)

    position = lax.broadcasted_iota(jnp.int32, (heads, tokens), 1)

    def attend_row(row):
        slot = lax.rem(row, SLOTS)
        keys = jnp.concatenate([key_buf[slot, k] for k in range(kv_heads)], axis=1)
        values = jnp.concatenate([value_buf[slot, k] for k in range(kv_heads)], axis=1)
        scores = lax.dot_general(
            query_buf[row].astype(jnp.bfloat16), keys, (((1,), (1,)), ((), ())),
            preferred_element_type=jnp.float32,
        )
        scores = jnp.where(position < length_ref[me, row], scores * scale, -1e30)
        weights = jnp.exp(scores - jnp.max(scores, axis=-1, keepdims=True))
        total = jnp.sum(weights, axis=-1, keepdims=True)
        full = jnp.dot(weights.astype(jnp.bfloat16), values, preferred_element_type=jnp.float32)
        mixed = jnp.concatenate(
            [
                full[k * group : (k + 1) * group, k * head_dim : (k + 1) * head_dim]
                for k in range(kv_heads)
            ],
            axis=0,
        )
        return mixed / total

    steps = rows // UNROLL

    @pl.loop(0, steps)
    def _(step):
        for u in range(UNROLL):
            each_page(step * UNROLL + u, lambda copy: copy.wait())
        results = [attend_row(step * UNROLL + u) for u in range(UNROLL)]
        for u in range(UNROLL):
            out_buf[step * UNROLL + u] = results[u]
        for u in range(UNROLL):
            @pl.when(step * UNROLL + u + SLOTS < rows)
            def _():
                each_page(step * UNROLL + u + SLOTS, lambda copy: copy.start())

        @pl.when(step == steps // 2)
        def _():
            def turn_move(move, index, live, pool_page, slot):
                @pl.when(live)
                def _():
                    for copy in load_move(move, index, pool_page):
                        copy.wait()
                    for copy in store_move(move, index, slot):
                        copy.start()

            each_move(turn_move)

    def end_move(move, index, live, pool_page, slot):
        for copy in clear_move(move, index, slot):
            copy.wait()

    for head in range(heads):
        out_ref[:, head * head_dim : (head + 1) * head_dim] = out_buf[:, head].astype(
            out_ref.dtype
        )

    each_move(end_move)


def attend(lengths, page_table, migration, dest_slots, queries, key_pages, value_pages):
    max_pages, _, rows = page_table.shape
    moves = migration.shape[1]
    kv_heads, _, page, head_dim = key_pages.shape
    heads = queries.shape[1] // head_dim
    area = jax.ShapeDtypeStruct((kv_heads, moves * max_pages, page, head_dim), key_pages.dtype)
    smem = pl.BlockSpec(memory_space=pltpu.SMEM)
    vmem = pl.BlockSpec(memory_space=pltpu.VMEM)
    hbm = pl.BlockSpec(memory_space=pl.ANY)
    return pl.pallas_call(
        attend_kernel,
        out_shape=(jax.ShapeDtypeStruct(queries.shape, queries.dtype), area, area),
        in_specs=[smem] * 4 + [vmem, hbm, hbm],
        out_specs=(vmem, hbm, hbm),
        scratch_shapes=[
            pltpu.VMEM((SLOTS, kv_heads, max_pages * page, head_dim), key_pages.dtype),
            pltpu.VMEM((SLOTS, kv_heads, max_pages * page, head_dim), key_pages.dtype),
            pltpu.VMEM((moves, max_pages, 2, kv_heads, page, head_dim), key_pages.dtype),
            pltpu.VMEM((kv_heads, page, head_dim), key_pages.dtype),
            pltpu.VMEM((rows, heads, kv_heads * head_dim), jnp.float32),
            pltpu.VMEM((rows, heads, head_dim), jnp.float32),
            pltpu.SemaphoreType.DMA((SLOTS, max_pages, 2)),
            pltpu.SemaphoreType.DMA((moves, max_pages, 2)),
        ],
        name="attend",
    )(lengths, page_table, migration, dest_slots, queries, key_pages, value_pages)


def project_kernel(
    pipes, tensors, attended_ref, weight_ref, out_ref,
    weight_buf, send_one, recv_one, own, send_two, recv_two,
    weight_sem, send_one_sem, recv_one_sem, send_two_sem, recv_two_sem,
):
    my_pipe = lax.axis_index("pipe")
    my_tensor = lax.axis_index("tensor")
    blocks = pipes * tensors
    width = out_ref.shape[1]

    def target(block):
        chunk, turn = block // tensors, lax.rem(block, tensors)
        to_pipe = lax.rem(my_pipe + pipes - 1 - chunk, pipes)
        to_tensor = lax.rem(my_tensor + 1 + turn, tensors)
        return chunk, turn, to_pipe, to_tensor

    def weight_copy(block):
        _, _, to_pipe, to_tensor = target(block)
        start = pl.multiple_of((to_pipe * tensors + to_tensor) * width, width)
        return pltpu.make_async_copy(
            weight_ref.at[:, pl.ds(start, width)], weight_buf.at[block], weight_sem.at[block]
        )

    def first_copy(chunk, turn, to_tensor):
        return pltpu.make_async_remote_copy(
            src_ref=send_one.at[chunk, turn],
            dst_ref=recv_one.at[chunk, turn],
            send_sem=send_one_sem.at[chunk, turn],
            recv_sem=recv_one_sem.at[chunk, turn],
            device_id={"tensor": to_tensor},
            device_id_type=MESH,
        )

    def second_copy(chunk, to_pipe):
        return pltpu.make_async_remote_copy(
            src_ref=send_two.at[chunk],
            dst_ref=recv_two.at[chunk],
            send_sem=send_two_sem.at[chunk],
            recv_sem=recv_two_sem.at[chunk],
            device_id={"pipe": to_pipe},
            device_id_type=MESH,
        )

    @pl.loop(0, blocks)
    def _(block):
        weight_copy(block).start()

    barrier = pltpu.get_barrier_semaphore()
    for step in range(1, tensors):
        pl.semaphore_signal(
            barrier, inc=1, device_id={"tensor": lax.rem(my_tensor + step, tensors)},
            device_id_type=MESH,
        )
    for step in range(1, pipes):
        pl.semaphore_signal(
            barrier, inc=1, device_id={"pipe": lax.rem(my_pipe + step, pipes)},
            device_id_type=MESH,
        )
    pl.semaphore_wait(barrier, tensors + pipes - 2)

    def gathered(chunk):
        total = own[chunk]
        for turn in range(tensors - 1):
            first_copy(chunk, turn, my_tensor).wait_recv()
            total = total + recv_one[chunk, turn].astype(jnp.float32)
        return total

    @pl.loop(0, blocks)
    def _(block):
        chunk, turn, _, to_tensor = target(block)
        weight_copy(block).wait()
        term = jnp.dot(
            attended_ref[...], weight_buf[block], preferred_element_type=jnp.float32
        )

        @pl.when(turn < tensors - 1)
        def _():
            send_one[chunk, turn] = term.astype(send_one.dtype)
            first_copy(chunk, turn, to_tensor).start()

        @pl.when(turn == tensors - 1)
        def _():
            own[chunk] = term

        @pl.when((turn == tensors - 1) & (chunk > 0))
        def _():
            before = chunk - 1
            send_two[before] = gathered(before).astype(send_two.dtype)
            second_copy(before, lax.rem(my_pipe + pipes - 1 - before, pipes)).start()

    total = gathered(pipes - 1)
    for chunk in range(pipes - 1):
        second_copy(chunk, my_pipe).wait_recv()
        total = total + recv_two[chunk].astype(jnp.float32)
    out_ref[...] = total.astype(out_ref.dtype)

    for chunk in range(pipes):
        for turn in range(tensors - 1):
            first_copy(chunk, turn, my_tensor).wait_send()
    for chunk in range(pipes - 1):
        second_copy(chunk, my_pipe).wait_send()


def project(attended, weight):
    pipes, tensors = lax.axis_size("pipe"), lax.axis_size("tensor")
    rows, depth = attended.shape
    columns = weight.shape[1]
    width = columns // (pipes * tensors)
    return pl.pallas_call(
        functools.partial(project_kernel, pipes, tensors),
        out_shape=jax.ShapeDtypeStruct((rows, width), jnp.bfloat16),
        in_specs=[pl.BlockSpec(memory_space=pltpu.VMEM), pl.BlockSpec(memory_space=pl.ANY)],
        out_specs=pl.BlockSpec(memory_space=pltpu.VMEM),
        scratch_shapes=[
            pltpu.VMEM((pipes * tensors, depth, width), weight.dtype),
            pltpu.VMEM((pipes, tensors - 1, rows, width), jnp.bfloat16),
            pltpu.VMEM((pipes, tensors - 1, rows, width), jnp.bfloat16),
            pltpu.VMEM((pipes, rows, width), jnp.float32),
            pltpu.VMEM((pipes - 1, rows, width), jnp.bfloat16),
            pltpu.VMEM((pipes - 1, rows, width), jnp.bfloat16),
            pltpu.SemaphoreType.DMA((pipes * tensors,)),
            pltpu.SemaphoreType.DMA((pipes, tensors - 1)),
            pltpu.SemaphoreType.DMA((pipes, tensors - 1)),
            pltpu.SemaphoreType.DMA((pipes - 1,)),
            pltpu.SemaphoreType.DMA((pipes - 1,)),
        ],
        cost_estimate=pl.CostEstimate(
            flops=2 * rows * depth * columns,
            bytes_accessed=2 * depth * columns,
            transcendentals=0,
        ),
        compiler_params=pltpu.CompilerParams(
            collective_id=0, has_side_effects=True, vmem_limit_bytes=48 * 1024 * 1024
        ),
        name="project",
    )(attended, weight)


def body(lengths, page_table, migration, dest_slots, queries, key_cache, value_cache, out_weight):
    kv_heads = key_cache.shape[2]
    head_dim = key_cache.shape[4]
    pool_pages = key_cache.shape[3] // PAGE
    key_pages = key_cache[0, 0].reshape(kv_heads, pool_pages, PAGE, head_dim)
    value_pages = value_cache[0, 0].reshape(kv_heads, pool_pages, PAGE, head_dim)
    attended, key_area, value_area = attend(
        lengths, page_table.transpose(2, 0, 1), migration.T, dest_slots.T, queries[0, 0],
        key_pages, value_pages,
    )
    got_keys, got_values = from_partner((key_area, value_area), "inst", 0)
    update = project(attended, out_weight[0])
    shape = (1, 1, kv_heads, got_keys.shape[1] * PAGE, head_dim)
    return (update[None], got_keys.reshape(shape), got_values.reshape(shape))


def solution(mesh):
    placed = (
        P(),
        P("inst", None, None),
        P(),
        P(),
        P("inst", "pipe", None, "tensor"),
        P("inst", "pipe", "tensor", None, None),
        P("inst", "pipe", "tensor", None, None),
        P("pipe", "tensor", None),
    )
    return jax.shard_map(
        body,
        mesh=mesh,
        in_specs=placed,
        out_specs=(
            P("inst", None, ("pipe", "tensor")),
            P("inst", "pipe", "tensor", None, None),
            P("inst", "pipe", "tensor", None, None),
        ),
        check_vma=False,
    )
```

```python
import functools
import math

import jax
import jax.numpy as jnp
from jax import lax
from jax.experimental import pallas as pl
from jax.experimental.pallas import tpu as pltpu
from jax.sharding import PartitionSpec as P

PAGE = 128
SLOTS = 16
UNROLL = 4
MESH = pl.DeviceIdType.MESH


def from_partner(array, axis, stride):
    return lax.ppermute(array, axis, [(i, i ^ 1 << stride) for i in range(lax.axis_size(axis))])


def attend_kernel(
    length_ref, table_ref, migration_ref, dest_ref, query_ref, key_ref, value_ref,
    out_ref, key_area, value_area,
    key_buf, value_buf, move_buf, zero_buf, query_buf, out_buf, page_sem, move_sem,
):
    max_pages, _, rows = table_ref.shape
    moves = migration_ref.shape[1]
    kv_heads, _, page, head_dim = key_ref.shape
    heads = query_ref.shape[1] // head_dim
    group = heads // kv_heads
    tokens = max_pages * page
    scale = 1.0 / math.sqrt(head_dim)
    me = lax.axis_index("inst")

    def page_copies(row, index):
        slot = lax.rem(row, SLOTS)
        source = table_ref[index, 0, row]
        place = pl.ds(index * page, page)
        return (
            pltpu.make_async_copy(
                key_ref.at[:, source], key_buf.at[slot, :, place], page_sem.at[slot, index, 0]
            ),
            pltpu.make_async_copy(
                value_ref.at[:, source], value_buf.at[slot, :, place], page_sem.at[slot, index, 1]
            ),
        )

    def each_page(row, act):
        for index in range(max_pages):
            @pl.when(index * page < length_ref[me, row])
            def _():
                for copy in page_copies(row, index):
                    act(copy)

    def each_move(act):
        @pl.loop(0, moves)
        def _(move):
            row, source = migration_ref[0, move], migration_ref[1, move]
            for index in range(max_pages):
                live = (source == me) & (index * page < length_ref[source, row])
                slot = dest_ref[index, move]
                act(move, index, live, table_ref[index, 0, row], slot)

    def load_move(move, index, pool_page):
        return [
            pltpu.make_async_copy(
                ref.at[:, pool_page], move_buf.at[move, index, which], move_sem.at[move, index, which]
            )
            for which, ref in enumerate((key_ref, value_ref))
        ]

    def store_move(move, index, slot):
        return [
            pltpu.make_async_copy(
                move_buf.at[move, index, which], area.at[:, slot], move_sem.at[move, index, which]
            )
            for which, area in enumerate((key_area, value_area))
        ]

    def clear_move(move, index, slot):
        return [
            pltpu.make_async_copy(zero_buf, area.at[:, slot], move_sem.at[move, index, which])
            for which, area in enumerate((key_area, value_area))
        ]

    zero_buf[...] = jnp.zeros_like(zero_buf)

    @pl.loop(0, SLOTS)
    def _(slot):
        value_buf[slot] = jnp.zeros(value_buf.shape[1:], value_buf.dtype)

    @pl.loop(0, SLOTS)
    def _(row):
        each_page(row, lambda copy: copy.start())

    def begin_move(move, index, live, pool_page, slot):
        @pl.when(live)
        def _():
            for copy in load_move(move, index, pool_page):
                copy.start()

        @pl.when(jnp.logical_not(live))
        def _():
            for copy in clear_move(move, index, slot):
                copy.start()

    each_move(begin_move)

    query_buf[...] = jnp.zeros_like(query_buf)
    for head in range(heads):
        own = head // group * head_dim
        query_buf[:, head, own : own + head_dim] = query_ref[
            :, head * head_dim : (head + 1) * head_dim
        ].astype(jnp.float32)

    position = lax.broadcasted_iota(jnp.int32, (heads, tokens), 1)

    def attend_row(row):
        slot = lax.rem(row, SLOTS)
        keys = jnp.concatenate([key_buf[slot, k] for k in range(kv_heads)], axis=1)
        values = jnp.concatenate([value_buf[slot, k] for k in range(kv_heads)], axis=1)
        scores = lax.dot_general(
            query_buf[row].astype(jnp.bfloat16), keys, (((1,), (1,)), ((), ())),
            preferred_element_type=jnp.float32,
        )
        scores = jnp.where(position < length_ref[me, row], scores * scale, -1e30)
        weights = jnp.exp(scores - jnp.max(scores, axis=-1, keepdims=True))
        total = jnp.sum(weights, axis=-1, keepdims=True)
        full = jnp.dot(weights.astype(jnp.bfloat16), values, preferred_element_type=jnp.float32)
        mixed = jnp.concatenate(
            [
                full[k * group : (k + 1) * group, k * head_dim : (k + 1) * head_dim]
                for k in range(kv_heads)
            ],
            axis=0,
        )
        return mixed / total

    steps = rows // UNROLL

    @pl.loop(0, steps)
    def _(step):
        for u in range(UNROLL):
            each_page(step * UNROLL + u, lambda copy: copy.wait())
        results = [attend_row(step * UNROLL + u) for u in range(UNROLL)]
        for u in range(UNROLL):
            out_buf[step * UNROLL + u] = results[u]
        for u in range(UNROLL):
            @pl.when(step * UNROLL + u + SLOTS < rows)
            def _():
                each_page(step * UNROLL + u + SLOTS, lambda copy: copy.start())

        @pl.when(step == steps // 2)
        def _():
            def turn_move(move, index, live, pool_page, slot):
                @pl.when(live)
                def _():
                    for copy in load_move(move, index, pool_page):
                        copy.wait()
                    for copy in store_move(move, index, slot):
                        copy.start()

            each_move(turn_move)

    def end_move(move, index, live, pool_page, slot):
        for copy in clear_move(move, index, slot):
            copy.wait()

    for head in range(heads):
        out_ref[:, head * head_dim : (head + 1) * head_dim] = out_buf[:, head].astype(
            out_ref.dtype
        )

    each_move(end_move)


def attend(lengths, page_table, migration, dest_slots, queries, key_pages, value_pages):
    max_pages, _, rows = page_table.shape
    moves = migration.shape[1]
    kv_heads, _, page, head_dim = key_pages.shape
    heads = queries.shape[1] // head_dim
    area = jax.ShapeDtypeStruct((kv_heads, moves * max_pages, page, head_dim), key_pages.dtype)
    smem = pl.BlockSpec(memory_space=pltpu.SMEM)
    vmem = pl.BlockSpec(memory_space=pltpu.VMEM)
    hbm = pl.BlockSpec(memory_space=pl.ANY)
    return pl.pallas_call(
        attend_kernel,
        out_shape=(pltpu.VMEM(queries.shape, queries.dtype), area, area),
        in_specs=[smem] * 4 + [vmem, hbm, hbm],
        out_specs=(vmem, hbm, hbm),
        scratch_shapes=[
            pltpu.VMEM((SLOTS, kv_heads, max_pages * page, head_dim), key_pages.dtype),
            pltpu.VMEM((SLOTS, kv_heads, max_pages * page, head_dim), key_pages.dtype),
            pltpu.VMEM((moves, max_pages, 2, kv_heads, page, head_dim), key_pages.dtype),
            pltpu.VMEM((kv_heads, page, head_dim), key_pages.dtype),
            pltpu.VMEM((rows, heads, kv_heads * head_dim), jnp.float32),
            pltpu.VMEM((rows, heads, head_dim), jnp.float32),
            pltpu.SemaphoreType.DMA((SLOTS, max_pages, 2)),
            pltpu.SemaphoreType.DMA((moves, max_pages, 2)),
        ],
        name="attend",
    )(lengths, page_table, migration, dest_slots, queries, key_pages, value_pages)


def project_kernel(
    pipes, tensors, attended_ref, weight_ref, out_ref,
    weight_buf, send_one, recv_one, own, send_two, recv_two,
    weight_sem, send_one_sem, recv_one_sem, send_two_sem, recv_two_sem,
):
    my_pipe = lax.axis_index("pipe")
    my_tensor = lax.axis_index("tensor")
    blocks = pipes * tensors
    width = out_ref.shape[1]

    def target(block):
        chunk, turn = block // tensors, lax.rem(block, tensors)
        to_pipe = lax.rem(my_pipe + pipes - 1 - chunk, pipes)
        to_tensor = lax.rem(my_tensor + 1 + turn, tensors)
        return chunk, turn, to_pipe, to_tensor

    def weight_copy(block):
        _, _, to_pipe, to_tensor = target(block)
        start = pl.multiple_of((to_pipe * tensors + to_tensor) * width, width)
        return pltpu.make_async_copy(
            weight_ref.at[:, pl.ds(start, width)], weight_buf.at[block], weight_sem.at[block]
        )

    def first_copy(chunk, turn, to_tensor):
        return pltpu.make_async_remote_copy(
            src_ref=send_one.at[chunk, turn],
            dst_ref=recv_one.at[chunk, turn],
            send_sem=send_one_sem.at[chunk, turn],
            recv_sem=recv_one_sem.at[chunk, turn],
            device_id={"tensor": to_tensor},
            device_id_type=MESH,
        )

    def second_copy(chunk, to_pipe):
        return pltpu.make_async_remote_copy(
            src_ref=send_two.at[chunk],
            dst_ref=recv_two.at[chunk],
            send_sem=send_two_sem.at[chunk],
            recv_sem=recv_two_sem.at[chunk],
            device_id={"pipe": to_pipe},
            device_id_type=MESH,
        )

    @pl.loop(0, blocks)
    def _(block):
        weight_copy(block).start()

    barrier = pltpu.get_barrier_semaphore()
    for step in range(1, tensors):
        pl.semaphore_signal(
            barrier, inc=1, device_id={"tensor": lax.rem(my_tensor + step, tensors)},
            device_id_type=MESH,
        )
    for step in range(1, pipes):
        pl.semaphore_signal(
            barrier, inc=1, device_id={"pipe": lax.rem(my_pipe + step, pipes)},
            device_id_type=MESH,
        )
    pl.semaphore_wait(barrier, tensors + pipes - 2)

    def gathered(chunk):
        total = own[chunk]
        for turn in range(tensors - 1):
            first_copy(chunk, turn, my_tensor).wait_recv()
            total = total + recv_one[chunk, turn].astype(jnp.float32)
        return total

    @pl.loop(0, blocks)
    def _(block):
        chunk, turn, _, to_tensor = target(block)
        weight_copy(block).wait()
        term = jnp.dot(
            attended_ref[...], weight_buf[block], preferred_element_type=jnp.float32
        )

        @pl.when(turn < tensors - 1)
        def _():
            send_one[chunk, turn] = term.astype(send_one.dtype)
            first_copy(chunk, turn, to_tensor).start()

        @pl.when(turn == tensors - 1)
        def _():
            own[chunk] = term

        @pl.when((turn == tensors - 1) & (chunk > 0))
        def _():
            before = chunk - 1
            send_two[before] = gathered(before).astype(send_two.dtype)
            second_copy(before, lax.rem(my_pipe + pipes - 1 - before, pipes)).start()

    total = gathered(pipes - 1)
    for chunk in range(pipes - 1):
        second_copy(chunk, my_pipe).wait_recv()
        total = total + recv_two[chunk].astype(jnp.float32)
    out_ref[...] = total.astype(out_ref.dtype)

    for chunk in range(pipes):
        for turn in range(tensors - 1):
            first_copy(chunk, turn, my_tensor).wait_send()
    for chunk in range(pipes - 1):
        second_copy(chunk, my_pipe).wait_send()


def project(attended, weight):
    pipes, tensors = lax.axis_size("pipe"), lax.axis_size("tensor")
    rows, depth = attended.shape
    columns = weight.shape[1]
    width = columns // (pipes * tensors)
    return pl.pallas_call(
        functools.partial(project_kernel, pipes, tensors),
        out_shape=jax.ShapeDtypeStruct((rows, width), jnp.bfloat16),
        in_specs=[pl.BlockSpec(memory_space=pltpu.VMEM), pl.BlockSpec(memory_space=pl.ANY)],
        out_specs=pl.BlockSpec(memory_space=pltpu.VMEM),
        scratch_shapes=[
            pltpu.VMEM((pipes * tensors, depth, width), weight.dtype),
            pltpu.VMEM((pipes, tensors - 1, rows, width), jnp.bfloat16),
            pltpu.VMEM((pipes, tensors - 1, rows, width), jnp.bfloat16),
            pltpu.VMEM((pipes, rows, width), jnp.float32),
            pltpu.VMEM((pipes - 1, rows, width), jnp.bfloat16),
            pltpu.VMEM((pipes - 1, rows, width), jnp.bfloat16),
            pltpu.SemaphoreType.DMA((pipes * tensors,)),
            pltpu.SemaphoreType.DMA((pipes, tensors - 1)),
            pltpu.SemaphoreType.DMA((pipes, tensors - 1)),
            pltpu.SemaphoreType.DMA((pipes - 1,)),
            pltpu.SemaphoreType.DMA((pipes - 1,)),
        ],
        cost_estimate=pl.CostEstimate(
            flops=2 * rows * depth * columns,
            bytes_accessed=2 * depth * columns,
            transcendentals=0,
        ),
        compiler_params=pltpu.CompilerParams(
            collective_id=0, has_side_effects=True, vmem_limit_bytes=48 * 1024 * 1024
        ),
        name="project",
    )(attended, weight)


def land_kernel(keys_ref, values_ref, key_out, value_out, sem):
    copies = [
        pltpu.make_async_copy(keys_ref, key_out, sem.at[0]),
        pltpu.make_async_copy(values_ref, value_out, sem.at[1]),
    ]
    for copy in copies:
        copy.start()
    for copy in copies:
        copy.wait()


def land(keys, values):
    shape = jax.ShapeDtypeStruct(keys.shape, keys.dtype)
    return pl.pallas_call(
        land_kernel,
        out_shape=(shape, shape),
        in_specs=[pl.BlockSpec(memory_space=pltpu.VMEM)] * 2,
        out_specs=[pl.BlockSpec(memory_space=pl.ANY)] * 2,
        scratch_shapes=[pltpu.SemaphoreType.DMA((2,))],
        compiler_params=pltpu.CompilerParams(vmem_limit_bytes=16 * 1024 * 1024),
        name="land",
    )(keys, values)


def body(lengths, page_table, migration, dest_slots, queries, key_cache, value_cache, out_weight):
    kv_heads = key_cache.shape[2]
    head_dim = key_cache.shape[4]
    pool_pages = key_cache.shape[3] // PAGE
    key_pages = key_cache[0, 0].reshape(kv_heads, pool_pages, PAGE, head_dim)
    value_pages = value_cache[0, 0].reshape(kv_heads, pool_pages, PAGE, head_dim)
    attended, key_area, value_area = attend(
        lengths, page_table.transpose(2, 0, 1), migration.T, dest_slots.T, queries[0, 0],
        key_pages, value_pages,
    )
    got_keys, got_values = from_partner((key_area, value_area), "inst", 0)
    update = project(attended, out_weight[0])
    got_keys, got_values = land(got_keys, got_values)
    shape = (1, 1, kv_heads, got_keys.shape[1] * PAGE, head_dim)
    return (update[None], got_keys.reshape(shape), got_values.reshape(shape))


def solution(mesh):
    placed = (
        P(),
        P("inst", None, None),
        P(),
        P(),
        P("inst", "pipe", None, "tensor"),
        P("inst", "pipe", "tensor", None, None),
        P("inst", "pipe", "tensor", None, None),
        P("pipe", "tensor", None),
    )
    return jax.shard_map(
        body,
        mesh=mesh,
        in_specs=placed,
        out_specs=(
            P("inst", None, ("pipe", "tensor")),
            P("inst", "pipe", "tensor", None, None),
            P("inst", "pipe", "tensor", None, None),
        ),
        check_vma=False,
    )
```
